32 devices in a mesh: mp: 2 (over x), dp: 16 (over z, y, core).
Axes of the slice: x: 2, y: 2, z: 4, core: 2. Of those that a mesh axis runs over, the one named last changes fastest.
Arguments:
- image: bfloat16 [16, 128, 1024], P('dp', 'mp'), may hold values from -8 to 8
- text: bfloat16 [2048, 1024], P('dp'), may hold values from -8 to 8
- logit_scale: float32 [1], replicated, may hold values from 10 to 30
Outputs:
- row_loss: float32 [16, 128], P('dp', 'mp')
- col_loss: float32 [16, 128], P('dp', 'mp')
The draws below stay inside these ranges and needn't reach their ends.
All inputs are finite; a program needn't handle non-finite values.
Results may differ from the reference program's by a relative error of at most 0.012.
Values may be sent and summed in bfloat16 or wider, within the bound.
A program may use at most 128 MiB of HBM per device.

```python
import math
import jax
import jax.numpy as jnp
from jax import lax

D = 1024
TOK_DEV = 128
TOKENS = 2048
N_DP = 16


def pair_rows(key):
    folded = jax.random.fold_in(key, 4099)
    subkeys = jax.random.split(folded, 7)
    groups = TOKENS // 8
    centers = jax.random.normal(subkeys[0], (groups, D), jnp.float32)
    members = jax.random.randint(subkeys[1], (TOKENS,), 0, groups)
    center_rows = centers[members]
    picture_pull = jax.random.uniform(subkeys[2], (TOKENS, 1), jnp.float32, minval=0.0, maxval=0.95)
    caption_pull = jax.random.uniform(subkeys[3], (TOKENS, 1), jnp.float32, minval=0.3, maxval=0.95)
    matching = jax.random.uniform(subkeys[4], (TOKENS, 1), jnp.float32, minval=0.0, maxval=0.7)
    picture_noise = jax.random.normal(subkeys[5], (TOKENS, D), jnp.float32)
    caption_noise = jax.random.normal(subkeys[6], (TOKENS, D), jnp.float32)
    picture = picture_pull * center_rows + jnp.sqrt(1.0 - picture_pull * picture_pull) * picture_noise
    caption_side = caption_pull * center_rows + jnp.sqrt(1.0 - caption_pull * caption_pull) * caption_noise
    caption = matching * picture + jnp.sqrt(1.0 - matching * matching) * caption_side
    return (jnp.clip(picture, -8.0, 8.0), jnp.clip(caption, -8.0, 8.0))


def draw_image(key, part):
    picture = pair_rows(key)[0]
    return picture.reshape(N_DP, TOK_DEV, D).astype(jnp.bfloat16)


def draw_text(key, part):
    caption = pair_rows(key)[1]
    return caption.astype(jnp.bfloat16)


def setup_inputs(seed: int = 0) -> dict:
    arg_keys = jax.random.split(jax.random.key(seed), 4)
    image = draw_image(jax.random.fold_in(arg_keys[3], 71), 0)
    text = draw_text(jax.random.fold_in(arg_keys[3], 71), 0)
    logit_scale = jnp.clip(jnp.exp(jax.random.uniform(arg_keys[2], (1,), jnp.float32, math.log(10.0), math.log(30.0))), 10.0, 30.0)
    return {"image": image, "text": text, "logit_scale": logit_scale}


def normalize(rows):
    wide = rows.astype(jnp.float32)
    return (wide * lax.rsqrt(lax.optimization_barrier(jnp.sum(wide * wide, axis=1, keepdims=True)) + 1e-06)).astype(jnp.bfloat16)

def reference(image, text, logit_scale):
    scale = logit_scale[0]
    img_n = normalize(image.reshape(TOKENS, D))
    text_n = normalize(text)
    diag = scale * lax.optimization_barrier(jnp.sum(img_n.astype(jnp.float32) * text_n.astype(jnp.float32), axis=1))
    block = TOK_DEV * 4
    blocks = img_n.reshape(TOKENS // block, block, D)

    def step(col_total, rows):
        scores = scale * jnp.dot(rows, text_n.T, preferred_element_type=jnp.float32)
        weights = jnp.exp(scores)
        return (col_total + lax.optimization_barrier(jnp.sum(weights, axis=0)), lax.optimization_barrier(jnp.sum(weights, axis=1)))
    col_total, row_total = lax.scan(step, jnp.zeros((TOKENS,), jnp.float32), blocks)
    row_total = row_total.reshape(TOKENS)
    row_loss = (jnp.log(row_total) - diag).reshape(N_DP, TOK_DEV)
    col_loss = (jnp.log(col_total) - diag).reshape(N_DP, TOK_DEV)
    return (row_loss, col_loss)
```

```python
import functools

import jax
import jax.numpy as jnp
from jax import lax
from jax.experimental import pallas as pl
from jax.experimental.pallas import tpu as pltpu
from jax.sharding import PartitionSpec as P

MESH = pl.DeviceIdType.MESH
F32 = jnp.float32


def normalize(raw):
    wide = raw.astype(F32)
    total = jnp.sum(wide * wide, axis=1, keepdims=True)
    return (wide * lax.rsqrt(total + 1e-06)).astype(jnp.bfloat16)


def lane_sums(values):
    folded = values[:, :128]
    for start in range(128, values.shape[1], 128):
        folded = folded + values[:, start : start + 128]
    return jnp.sum(folded.T, axis=0, keepdims=True)


def flipped(index, mask):
    bit = 1
    while bit <= mask:
        if mask & bit:
            index = index + bit * (1 - 2 * (index // bit % 2))
        bit *= 2
    return index


def kernel(
    groups, run, ring,
    scale_ref, image_ref, text_ref, row_ref, col_ref,
    img_raw, txt_raw, img_n, txt_n, weights_col, row_out, row_in, col_out, col_in,
    local_sem, img_send, img_recv, txt_send, txt_recv, row_send, row_recv, col_send, col_recv,
):
    group = lax.axis_index("mp")
    me = lax.axis_index("dp")
    rows = image_ref.shape[0]
    cols = text_ref.shape[0]
    half = rows // 2
    lane = me % run
    spot = me // run

    def along(step):
        return ((spot + step + ring) % ring) * run + lane

    def remote(src, dst, send, recv, dp, mp=None):
        where = {"dp": dp} if mp is None else {"dp": dp, "mp": mp}
        return pltpu.make_async_remote_copy(
            src_ref=src, dst_ref=dst, send_sem=send, recv_sem=recv,
            device_id=where, device_id_type=MESH,
        )

    load_img = pltpu.make_async_copy(image_ref, img_raw.at[0], local_sem.at[0])
    load_txt = pltpu.make_async_copy(text_ref, txt_raw.at[0], local_sem.at[1])
    load_img.start()
    load_txt.start()

    barrier = pltpu.get_barrier_semaphore()
    greeted = 0
    for step in range(1, ring):
        pl.semaphore_signal(barrier, inc=1, device_id={"dp": along(step)}, device_id_type=MESH)
        greeted += 1
    for k in range(run):
        for m in range(groups):
            if k or m:
                pl.semaphore_signal(
                    barrier, inc=1, device_id_type=MESH,
                    device_id={"dp": flipped(me, k), "mp": (group + m) % groups},
                )
                greeted += 1
    pl.semaphore_wait(barrier, greeted)

    def img_copy(way, step, part):
        held = (ring - (step - 1)) % ring if way == 0 else step - 1
        lands = ring - step if way == 0 else step
        span = pl.ds(part * half, half)
        src = image_ref.at[span] if step == 1 else img_raw.at[held, span]
        return remote(
            src, img_raw.at[lands, span],
            img_send.at[way, step - 1, part], img_recv.at[way, step - 1, part],
            along(1 if way == 0 else -1),
        )

    last = ring // 2
    img_copies = {}
    for step in range(1, last + 1):
        for way in range(2):
            for part in ((0, 1) if way == 0 else (1, 0)):
                if step < last or part == way:
                    img_copies[way, step, part] = img_copy(way, step, part)

    def txt_copy(slot):
        bit = slot & -slot
        held = slot - bit
        src = text_ref if held == 0 else txt_raw.at[held]
        return remote(
            src, txt_raw.at[slot], txt_send.at[slot - 1], txt_recv.at[slot - 1],
            flipped(me, bit),
        )

    txt_copies = {slot: txt_copy(slot) for slot in range(1, run)}

    for key in img_copies:
        if key[1] == 1:
            img_copies[key].start()
    for slot in reversed(range(1, run)):
        if slot & (slot - 1) == 0:
            txt_copies[slot].start()

    scale = scale_ref[0]
    load_img.wait()
    load_txt.wait()
    img_n[0] = normalize(img_raw[0])
    txt_n[pl.ds(0, cols)] = normalize(txt_raw[0])
    own = txt_n[pl.ds(pl.multiple_of(group * rows, rows), rows)]
    diag = scale * lane_sums(img_n[0].astype(F32) * own.astype(F32))

    def img_arrive(way, step, part):
        img_copies[way, step, part].wait_recv()
        if (way, step + 1, part) in img_copies:
            img_copies[way, step + 1, part].start()

    for step in range(1, last):
        for order in range(2):
            for way in range(2):
                img_arrive(way, step, way if order == 0 else 1 - way)
        for slot in (step, ring - step):
            img_n[slot] = normalize(img_raw[slot])

    for bit in reversed(range(run.bit_length() - 1)):
        for slot in range(1, run):
            if slot & -slot == 1 << bit:
                txt_copies[slot].wait_recv()
                for low in range(bit):
                    txt_copies[slot + (1 << low)].start()
                txt_n[pl.ds(slot * cols, cols)] = normalize(txt_raw[slot])
    for way in range(2):
        img_arrive(way, last, way)
    img_n[last] = normalize(img_raw[last])

    order = [0]
    for step in range(1, last):
        order += [step, ring - step]
    order.append(last)
    row_copies = []
    for turn, slot in enumerate(order):
        scores = scale * lax.dot_general(
            img_n[slot], txt_n[...], (((1,), (1,)), ((), ())), preferred_element_type=F32
        )
        weights = jnp.exp(scores)
        sums = lane_sums(weights)
        if slot == 0:
            row_in[0, :, :rows] = jnp.broadcast_to(sums, (8, rows))
        else:
            row_out[slot, :, :rows] = jnp.broadcast_to(sums, (8, rows))
            copy = remote(
                row_out.at[slot], row_in.at[ring - slot],
                row_send.at[slot - 1], row_recv.at[ring - slot - 1], along(slot),
            )
            copy.start()
            row_copies.append(copy)
        part = jnp.sum(weights, axis=0, keepdims=True)
        weights_col[...] = part if turn == 0 else weights_col[...] + part

    col_copies = []
    for k in range(run):
        col_out[k] = jnp.broadcast_to(weights_col[:, k * cols : (k + 1) * cols], (8, cols))
        for m in range(groups):
            if k or m:
                copy = remote(
                    col_out.at[k], col_in.at[k * groups + (groups - m) % groups],
                    col_send.at[k * groups + m], col_recv.at[k * groups + (groups - m) % groups],
                    flipped(me, k), (group + m) % groups,
                )
                copy.start()
                col_copies.append(copy)
    row_total = row_in[0, :1, :rows]
    for copy in row_copies:
        copy.wait_recv()
    for slot in range(1, ring):
        row_total = row_total + row_in[slot, :1, :rows]
    row_ref[...] = jnp.log(row_total) - diag
    for copy in col_copies:
        copy.wait_recv()
    col_total = col_out[0, :1]
    for slot in range(1, run * groups):
        col_total = col_total + col_in[slot, :1]
    col_own = col_total[:, :rows]
    for g in range(1, groups):
        col_own = jnp.where(group == g, col_total[:, g * rows : (g + 1) * rows], col_own)
    col_ref[...] = jnp.log(col_own) - diag
    for copy in [*img_copies.values(), *txt_copies.values(), *row_copies, *col_copies]:
        copy.wait_send()


def solution(mesh):
    groups, n = mesh.shape["mp"], mesh.shape["dp"]
    run = 1 << ((n.bit_length() - 1) // 2)
    ring = n // run

    def on_device(image, text, logit_scale):
        _, rows, depth = image.shape
        cols = text.shape[0]
        vmem = pl.BlockSpec(memory_space=pltpu.VMEM)
        hbm = pl.BlockSpec(memory_space=pl.ANY)
        dma = pltpu.SemaphoreType.DMA
        out = jax.ShapeDtypeStruct((1, rows), F32)
        return pl.pallas_call(
            functools.partial(kernel, groups, run, ring),
            out_shape=(out, out),
            in_specs=[pl.BlockSpec(memory_space=pltpu.SMEM), hbm, hbm],
            out_specs=(vmem, vmem),
            scratch_shapes=[
                pltpu.VMEM((ring, rows, depth), jnp.bfloat16),
                pltpu.VMEM((run, cols, depth), jnp.bfloat16),
                pltpu.VMEM((ring, rows, depth), jnp.bfloat16),
                pltpu.VMEM((run * cols, depth), jnp.bfloat16),
                pltpu.VMEM((1, run * cols), F32),
                pltpu.VMEM((ring, 8, 128), F32),
                pltpu.VMEM((ring, 8, 128), F32),
                pltpu.VMEM((run, 8, cols), F32),
                pltpu.VMEM((run * groups, 8, cols), F32),
                dma((2,)),
                dma((2, ring // 2, 2)),
                dma((2, ring // 2, 2)),
                dma((run - 1,)),
                dma((run - 1,)),
                dma((ring - 1,)),
                dma((ring - 1,)),
                dma((run * groups,)),
                dma((run * groups,)),
            ],
            compiler_params=pltpu.CompilerParams(collective_id=0, has_side_effects=True),
        )(logit_scale, image.reshape(rows, depth), text)

    return jax.shard_map(
        on_device,
        mesh=mesh,
        in_specs=(P("dp", "mp", None), P("dp", None), P()),
        out_specs=(P("dp", "mp"), P("dp", "mp")),
        check_vma=False,
    )
```

```python
import functools

import jax
import jax.numpy as jnp
from jax import lax
from jax.experimental import pallas as pl
from jax.experimental.pallas import tpu as pltpu
from jax.sharding import PartitionSpec as P

MESH = pl.DeviceIdType.MESH
F32 = jnp.float32
IMG_PARTS = 4
TXT_PARTS = 2


def normalize(raw):
    wide = raw.astype(F32)
    total = jnp.sum(wide * wide, axis=1, keepdims=True)
    return (wide * lax.rsqrt(total + 1e-06)).astype(jnp.bfloat16)


def lane_sums(values):
    folded = values[:, :128]
    for start in range(128, values.shape[1], 128):
        folded = folded + values[:, start : start + 128]
    return jnp.sum(folded.T, axis=0, keepdims=True)


def low_bit(slot):
    return slot & -slot


def by_level(slots):
    return sorted((s for s in slots if s), key=lambda s: (-low_bit(s), s))


def kernel(
    groups, txt_bits, img_bits,
    scale_ref, image_ref, text_ref, out_ref,
    img_raw, txt_raw, img_n, txt_n, weights_col, row_out, row_in, col_out, col_in,
    local_sem, img_send, img_recv, own_send, own_recv, hop_send, hop_recv,
    mp_send, mp_recv, core_send, core_recv, row_send, row_recv, col_send, col_recv,
):
    group = lax.axis_index("mp")
    me = lax.axis_index("dp")
    rows = image_ref.shape[0]
    cols = text_ref.shape[0]
    n_img, n_txt = 1 << len(img_bits), 1 << len(txt_bits)

    def peer(slot, bits):
        place = me
        for i, bit in enumerate(bits):
            if slot >> i & 1:
                place = place + (1 - 2 * (me // (1 << bit) % 2)) * (1 << bit)
        return place

    def other(m):
        return (group + m) % groups

    def remote(src, dst, send, recv, dp=None, mp=None):
        where = {}
        if dp is not None:
            where["dp"] = dp
        if mp is not None:
            where["mp"] = mp
        return pltpu.make_async_remote_copy(
            src_ref=src, dst_ref=dst, send_sem=send, recv_sem=recv,
            device_id=where, device_id_type=MESH,
        )

    load_img = pltpu.make_async_copy(image_ref, img_raw.at[0], local_sem.at[0])
    load_txt = pltpu.make_async_copy(text_ref, txt_raw.at[0], local_sem.at[1])
    load_img.start()
    load_txt.start()

    barrier = pltpu.get_barrier_semaphore()
    greeted = 0
    for slot in range(1, n_img):
        pl.semaphore_signal(
            barrier, inc=1, device_id={"dp": peer(slot, img_bits)}, device_id_type=MESH
        )
        greeted += 1
    for slot in range(n_txt):
        for m in range(groups):
            if slot or m:
                pl.semaphore_signal(
                    barrier, inc=1, device_id_type=MESH,
                    device_id={"dp": peer(slot, txt_bits), "mp": other(m)},
                )
                greeted += 1
    pl.semaphore_wait(barrier, greeted)
    sent = []

    def start(copy):
        copy.start()
        sent.append(copy)

    img_chunk = rows // IMG_PARTS
    txt_chunk = rows // TXT_PARTS

    def img_copy(slot, part):
        span = pl.ds(part * img_chunk, img_chunk)
        held = slot - low_bit(slot)
        src = img_raw.at[held, span] if held else image_ref.at[span]
        return remote(
            src, img_raw.at[slot, span],
            img_send.at[slot - 1, part], img_recv.at[slot - 1, part],
            peer(low_bit(slot), img_bits),
        )

    def piece(m, part):
        first = (group - m + groups) % groups * rows + part * txt_chunk
        return pl.ds(pl.multiple_of(first, txt_chunk), txt_chunk)

    def hop_copy(slot, part):
        held = slot - low_bit(slot)
        span = piece(0, part)
        src = txt_raw.at[held, span] if held else text_ref.at[span]
        return remote(
            src, txt_raw.at[slot, span],
            hop_send.at[slot, part], hop_recv.at[slot, part],
            peer(low_bit(slot), txt_bits),
        )

    def mp_copy(slot, m, part):
        span = piece(0, part)
        return remote(
            txt_raw.at[slot, span], txt_raw.at[slot, span],
            mp_send.at[slot, m, part], mp_recv.at[slot, m, part], mp=other(m),
        )

    def core_copy(slot, m, part):
        span = piece(m, part)
        return remote(
            txt_raw.at[slot, span], txt_raw.at[slot + 1, span],
            core_send.at[slot, m, part], core_recv.at[slot, m, part], peer(1, txt_bits),
        )

    own_copy = remote(
        text_ref, txt_raw.at[1], own_send.at[0], own_recv.at[0], peer(1, txt_bits)
    )
    even = by_level(range(0, n_txt, 2))
    img_order = by_level(range(n_img))

    for slot in even:
        if slot == low_bit(slot):
            for part in range(TXT_PARTS):
                start(hop_copy(slot, part))
    for slot in img_order:
        if slot == low_bit(slot):
            for part in range(IMG_PARTS):
                start(img_copy(slot, part))
    start(own_copy)

    scale = scale_ref[0]
    load_img.wait()
    load_txt.wait()
    img_n[0] = normalize(img_raw[0])
    txt_n[pl.ds(0, cols)] = normalize(txt_raw[0])
    own = txt_n[pl.ds(pl.multiple_of(group * rows, rows), rows)]
    diag = scale * lane_sums(img_n[0].astype(F32) * own.astype(F32))
    own_copy.wait_recv()
    txt_n[pl.ds(cols, cols)] = normalize(txt_raw[1])

    def text_block(slot):
        txt_n[pl.ds(slot * cols, cols)] = normalize(txt_raw[slot])

    for slot in even:
        for part in range(TXT_PARTS):
            hop_copy(slot, part).wait_recv()
            bit = 2
            while bit < low_bit(slot):
                start(hop_copy(slot + bit, part))
                bit *= 2
            for m in range(1, groups):
                start(mp_copy(slot, m, part))
            start(core_copy(slot, 0, part))

    def img_arrive(slot, part):
        img_copy(slot, part).wait_recv()
        bit = 1
        while bit < low_bit(slot):
            start(img_copy(slot + bit, part))
            bit *= 2

    def img_block(slot):
        img_n[slot] = normalize(img_raw[slot])

    final = img_order[-1]
    early = [s for s in img_order if s == 1]
    passed = [s for s in img_order if s not in early and s != final]
    text_waits = [(slot, m, part) for slot in even for part in range(TXT_PARTS) for m in range(1, groups)]
    image_waits = [(slot, part) for slot in passed for part in range(IMG_PARTS)]
    for slot in early:
        for part in range(IMG_PARTS):
            img_arrive(slot, part)
        if slot != final:
            img_block(slot)
    share = -(-len(image_waits) // max(len(text_waits), 1))
    for i in range(max(len(text_waits), 1)):
        for slot, m, part in text_waits[i : i + 1]:
            mp_copy(slot, m, part).wait_recv()
            start(core_copy(slot, m, part))
        for slot, part in image_waits[i * share : (i + 1) * share]:
            img_arrive(slot, part)
    for slot in even:
        text_block(slot)
    for slot in passed:
        img_block(slot)
    for slot in even:
        for m in range(groups):
            for part in range(TXT_PARTS):
                core_copy(slot, m, part).wait_recv()
        text_block(slot + 1)

    row_copies = []

    def image_rows(slot, first):
        scores = scale * lax.dot_general(
            img_n[slot], txt_n[...], (((1,), (1,)), ((), ())), preferred_element_type=F32
        )
        weights = jnp.exp(scores)
        sums = jnp.broadcast_to(lane_sums(weights), (8, rows))
        if slot == 0:
            row_in[0, :, :rows] = sums
        else:
            row_out[slot, :, :rows] = sums
            copy = remote(
                row_out.at[slot], row_in.at[slot],
                row_send.at[slot - 1], row_recv.at[slot - 1], peer(slot, img_bits),
            )
            start(copy)
            row_copies.append(copy)
        part = jnp.sum(weights, axis=0, keepdims=True)
        weights_col[...] = part if first else weights_col[...] + part

    for slot in [0, *early, *passed]:
        if slot != final:
            image_rows(slot, slot == 0)
    if final not in early:
        for part in range(IMG_PARTS):
            img_arrive(final, part)
    img_block(final)
    image_rows(final, False)

    col_copies = []
    for slot in range(n_txt):
        col_out[slot] = jnp.broadcast_to(
            weights_col[:, slot * cols : (slot + 1) * cols], (8, cols)
        )
        for m in range(groups):
            if slot or m:
                to = slot * groups + (groups - m) % groups
                copy = remote(
                    col_out.at[slot], col_in.at[to],
                    col_send.at[slot * groups + m], col_recv.at[to],
                    peer(slot, txt_bits), other(m),
                )
                start(copy)
                col_copies.append(copy)
    row_total = row_in[0, :1, :rows]
    for copy in row_copies:
        copy.wait_recv()
    for slot in range(1, n_img):
        row_total = row_total + row_in[slot, :1, :rows]
    for copy in col_copies:
        copy.wait_recv()
    col_total = col_out[0, :1]
    for slot in range(1, n_txt * groups):
        col_total = col_total + col_in[slot, :1]
    col_own = col_total[:, :rows]
    for g in range(1, groups):
        col_own = jnp.where(group == g, col_total[:, g * rows : (g + 1) * rows], col_own)
    out_ref[0:1] = row_total
    out_ref[1:2] = col_own
    out_ref[2:3] = diag
    for copy in sent:
        copy.wait_send()


def solution(mesh):
    groups, n = mesh.shape["mp"], mesh.shape["dp"]
    levels = n.bit_length() - 1
    txt_bits = list(range(0, levels, 2))
    img_bits = list(range(1, levels, 2))
    n_txt, n_img = 1 << len(txt_bits), 1 << len(img_bits)

    def on_device(image, text, logit_scale):
        _, rows, depth = image.shape
        cols = text.shape[0]
        hbm = pl.BlockSpec(memory_space=pl.ANY)
        dma = pltpu.SemaphoreType.DMA
        totals = pl.pallas_call(
            functools.partial(kernel, groups, txt_bits, img_bits),
            out_shape=jax.ShapeDtypeStruct((3, rows), F32),
            in_specs=[pl.BlockSpec(memory_space=pltpu.SMEM), hbm, hbm],
            out_specs=pl.BlockSpec(memory_space=pltpu.VMEM),
            scratch_shapes=[
                pltpu.VMEM((n_img, rows, depth), jnp.bfloat16),
                pltpu.VMEM((n_txt, cols, depth), jnp.bfloat16),
                pltpu.VMEM((n_img, rows, depth), jnp.bfloat16),
                pltpu.VMEM((n_txt * cols, depth), jnp.bfloat16),
                pltpu.VMEM((1, n_txt * cols), F32),
                pltpu.VMEM((n_img, 8, 128), F32),
                pltpu.VMEM((n_img, 8, 128), F32),
                pltpu.VMEM((n_txt, 8, cols), F32),
                pltpu.VMEM((n_txt * groups, 8, cols), F32),
                dma((2,)),
                dma((n_img - 1, IMG_PARTS)),
                dma((n_img - 1, IMG_PARTS)),
                dma((1,)),
                dma((1,)),
                dma((n_txt, TXT_PARTS)),
                dma((n_txt, TXT_PARTS)),
                dma((n_txt, groups, TXT_PARTS)),
                dma((n_txt, groups, TXT_PARTS)),
                dma((n_txt, groups, TXT_PARTS)),
                dma((n_txt, groups, TXT_PARTS)),
                dma((n_img - 1,)),
                dma((n_img - 1,)),
                dma((n_txt * groups,)),
                dma((n_txt * groups,)),
            ],
            compiler_params=pltpu.CompilerParams(collective_id=0, has_side_effects=True),
        )(logit_scale, image.reshape(rows, depth), text)
        row_loss = jnp.log(totals[0:1]) - totals[2:3]
        col_loss = jnp.log(totals[1:2]) - totals[2:3]
        return (row_loss, col_loss)

    return jax.shard_map(
        on_device,
        mesh=mesh,
        in_specs=(P("dp", "mp", None), P("dp", None), P()),
        out_specs=(P("dp", "mp"), P("dp", "mp")),
        check_vma=False,
    )
```

```python
import functools

import jax
import jax.numpy as jnp
from jax import lax
from jax.experimental import pallas as pl
from jax.experimental.pallas import tpu as pltpu
from jax.sharding import PartitionSpec as P

MESH = pl.DeviceIdType.MESH
F32 = jnp.float32
IMG_PARTS = 4
TXT_PARTS = 2


def normalize(raw):
    wide = raw.astype(F32)
    total = jnp.sum(wide * wide, axis=1, keepdims=True)
    return (wide * lax.rsqrt(total + 1e-06)).astype(jnp.bfloat16)


def lane_sums(values):
    folded = values[:, :128]
    for start in range(128, values.shape[1], 128):
        folded = folded + values[:, start : start + 128]
    return jnp.sum(folded.T, axis=0, keepdims=True)


def flipped(index, mask):
    bit = 1
    while bit <= mask:
        if mask & bit:
            index = index + bit * (1 - 2 * (index // bit % 2))
        bit *= 2
    return index


def kernel(
    groups, run, ring,
    scale_ref, image_ref, text_ref, out_ref,
    image_own, img_raw, txt_raw, img_n, txt_n, weights_col, row_out, row_in, col_out, col_in,
    local_sem, img_send, img_recv, txt_send, txt_recv, row_send, row_recv, col_send, col_recv,
):
    group = lax.axis_index("mp")
    me = lax.axis_index("dp")
    rows = image_ref.shape[0]
    cols = text_ref.shape[0]
    lane = me % run
    spot = me // run

    def along(step):
        return ((spot + step + ring) % ring) * run + lane

    def remote(src, dst, send, recv, dp, mp=None):
        where = {"dp": dp} if mp is None else {"dp": dp, "mp": mp}
        return pltpu.make_async_remote_copy(
            src_ref=src, dst_ref=dst, send_sem=send, recv_sem=recv,
            device_id=where, device_id_type=MESH,
        )

    load_img = pltpu.make_async_copy(image_ref, image_own, local_sem.at[0])
    load_txt = pltpu.make_async_copy(text_ref, txt_raw.at[0], local_sem.at[1])
    load_img.start()
    load_txt.start()

    barrier = pltpu.get_barrier_semaphore()
    greeted = 0
    for step in range(1, ring):
        pl.semaphore_signal(barrier, inc=1, device_id={"dp": along(step)}, device_id_type=MESH)
        greeted += 1
    for k in range(run):
        for m in range(groups):
            if k or m:
                pl.semaphore_signal(
                    barrier, inc=1, device_id_type=MESH,
                    device_id={"dp": flipped(me, k), "mp": (group + m) % groups},
                )
                greeted += 1
    pl.semaphore_wait(barrier, greeted)

    part_rows = rows // IMG_PARTS
    img_sent = []

    def img_copy(way, source, part, own=False):
        span = pl.ds(part * part_rows, part_rows)
        return remote(
            image_ref.at[span] if own else img_raw.at[source, span],
            img_raw.at[source, span],
            img_send.at[way, source, part], img_recv.at[source, part],
            along(1 - 2 * way),
        )

    def pass_on(source, part, own=False):
        for way in range(2):
            if own:
                goes = spot < ring - 1 if way == 0 else spot > 0
            elif way == 0:
                goes = jnp.logical_and(source < spot, spot < ring - 1)
            else:
                goes = jnp.logical_and(source > spot, spot > 0)
            copy = img_copy(way, source, part, own)
            img_sent.append((goes, copy))

            @pl.when(goes)
            def _():
                copy.start()

    short = jnp.minimum(spot, ring - 1 - spot)
    ahead = jnp.where(spot < ring - 1 - spot, 1, -1)

    def nearest(turn):
        both = (turn + 1) // 2 * (1 - 2 * (turn % 2))
        return spot + jnp.where(turn <= 2 * short, both, ahead * (turn - short))

    txt_rows = cols // TXT_PARTS

    def txt_copy(slot, part):
        bit = slot & -slot
        held = slot - bit
        span = pl.ds(part * txt_rows, txt_rows)
        return remote(
            txt_raw.at[held, span] if held else text_ref.at[span],
            txt_raw.at[slot, span],
            txt_send.at[slot - 1, part], txt_recv.at[slot - 1, part], flipped(me, bit),
        )

    txt_sent = []

    def txt_start(slot, part):
        copy = txt_copy(slot, part)
        copy.start()
        txt_sent.append(copy)

    def txt_arrive(slot, part):
        txt_copy(slot, part).wait_recv()
        bit = 1
        while bit < slot & -slot:
            txt_start(slot + bit, part)
            bit *= 2

    def txt_block(slot):
        txt_n[pl.ds(slot * cols, cols)] = normalize(txt_raw[slot])

    for part in range(IMG_PARTS):
        pass_on(spot, part, True)
    for slot in reversed(range(1, run)):
        if slot & (slot - 1) == 0:
            for part in range(TXT_PARTS):
                txt_start(slot, part)

    scale = scale_ref[0]
    load_img.wait()
    load_txt.wait()
    img_n[0] = normalize(image_own[...])
    txt_n[pl.ds(0, cols)] = normalize(txt_raw[0])
    own = txt_n[pl.ds(pl.multiple_of(group * rows, rows), rows)]
    diag = scale * lane_sums(img_n[0].astype(F32) * own.astype(F32))

    def img_arrive(turn, part):
        source = nearest(turn)
        img_copy(0, source, part).wait_recv()
        pass_on(source, part)

    def img_block(turn):
        img_n[turn] = normalize(img_raw[nearest(turn)])

    txt_order = sorted(range(1, run), key=lambda k: -(k & -k))
    txt_waits = [(slot, part) for slot in txt_order if slot % 2 == 0 for part in range(TXT_PARTS)]
    img_waits = [(turn, part) for turn in range(1, ring - 1) for part in range(IMG_PARTS)]
    lead = min(IMG_PARTS, len(img_waits))
    for turn, part in img_waits[:lead]:
        img_arrive(turn, part)
    rest = img_waits[lead:]
    share = -(-len(rest) // max(len(txt_waits), 1))
    for i in range(max(len(txt_waits), 1)):
        for slot, part in txt_waits[i : i + 1]:
            txt_arrive(slot, part)
        for turn, part in rest[i * share : (i + 1) * share]:
            img_arrive(turn, part)
    for slot in txt_order:
        if slot % 2 == 0:
            txt_block(slot)
    for turn in range(1, ring - 1):
        img_block(turn)
    for slot in txt_order:
        if slot % 2:
            for part in range(TXT_PARTS):
                txt_arrive(slot, part)
            txt_block(slot)

    row_copies = []

    def image_rows(turn):
        scores = scale * lax.dot_general(
            img_n[turn], txt_n[...], (((1,), (1,)), ((), ())), preferred_element_type=F32
        )
        weights = jnp.exp(scores)
        sums = jnp.broadcast_to(lane_sums(weights), (8, rows))
        if turn == 0:
            row_in[spot, :, :rows] = sums
        else:
            row_out[turn, :, :rows] = sums
            copy = remote(
                row_out.at[turn], row_in.at[spot],
                row_send.at[turn - 1], row_recv.at[spot],
                nearest(turn) * run + lane,
            )
            copy.start()
            row_copies.append(copy)
        part = jnp.sum(weights, axis=0, keepdims=True)
        weights_col[...] = part if turn == 0 else weights_col[...] + part

    for turn in range(ring - 1):
        image_rows(turn)
    for part in range(IMG_PARTS):
        img_arrive(ring - 1, part)
    img_block(ring - 1)
    image_rows(ring - 1)

    col_copies = []
    for k in range(run):
        col_out[k] = jnp.broadcast_to(weights_col[:, k * cols : (k + 1) * cols], (8, cols))
        for m in range(groups):
            if k or m:
                to = k * groups + (groups - m) % groups
                copy = remote(
                    col_out.at[k], col_in.at[to],
                    col_send.at[k * groups + m], col_recv.at[to],
                    flipped(me, k), (group + m) % groups,
                )
                copy.start()
                col_copies.append(copy)
    for turn in range(1, ring):
        source = nearest(turn)
        remote(
            row_out.at[turn], row_in.at[source], row_send.at[turn - 1], row_recv.at[source],
            source * run + lane,
        ).wait_recv()
    row_total = row_in[0, :1, :rows]
    for slot in range(1, ring):
        row_total = row_total + row_in[slot, :1, :rows]
    for copy in col_copies:
        copy.wait_recv()
    col_total = col_out[0, :1]
    for slot in range(1, run * groups):
        col_total = col_total + col_in[slot, :1]
    col_own = col_total[:, :rows]
    for g in range(1, groups):
        col_own = jnp.where(group == g, col_total[:, g * rows : (g + 1) * rows], col_own)
    out_ref[0:1] = row_total
    out_ref[1:2] = col_own
    out_ref[2:3] = diag
    for goes, copy in img_sent:

        @pl.when(goes)
        def _():
            copy.wait_send()

    for copy in [*txt_sent, *row_copies, *col_copies]:
        copy.wait_send()


def solution(mesh):
    groups, n = mesh.shape["mp"], mesh.shape["dp"]
    run = 1 << ((n.bit_length() - 1) // 2)
    ring = n // run

    def on_device(image, text, logit_scale):
        _, rows, depth = image.shape
        cols = text.shape[0]
        hbm = pl.BlockSpec(memory_space=pl.ANY)
        dma = pltpu.SemaphoreType.DMA
        totals = pl.pallas_call(
            functools.partial(kernel, groups, run, ring),
            out_shape=jax.ShapeDtypeStruct((3, rows), F32),
            in_specs=[pl.BlockSpec(memory_space=pltpu.SMEM), hbm, hbm],
            out_specs=pl.BlockSpec(memory_space=pltpu.VMEM),
            scratch_shapes=[
                pltpu.VMEM((rows, depth), jnp.bfloat16),
                pltpu.VMEM((ring, rows, depth), jnp.bfloat16),
                pltpu.VMEM((run, cols, depth), jnp.bfloat16),
                pltpu.VMEM((ring, rows, depth), jnp.bfloat16),
                pltpu.VMEM((run * cols, depth), jnp.bfloat16),
                pltpu.VMEM((1, run * cols), F32),
                pltpu.VMEM((ring, 8, 128), F32),
                pltpu.VMEM((ring, 8, 128), F32),
                pltpu.VMEM((run, 8, cols), F32),
                pltpu.VMEM((run * groups, 8, cols), F32),
                dma((2,)),
                dma((2, ring, IMG_PARTS)),
                dma((ring, IMG_PARTS)),
                dma((run - 1, TXT_PARTS)),
                dma((run - 1, TXT_PARTS)),
                dma((ring - 1,)),
                dma((ring,)),
                dma((run * groups,)),
                dma((run * groups,)),
            ],
            compiler_params=pltpu.CompilerParams(collective_id=0, has_side_effects=True),
        )(logit_scale, image.reshape(rows, depth), text)
        row_loss = jnp.log(totals[0:1]) - totals[2:3]
        col_loss = jnp.log(totals[1:2]) - totals[2:3]
        return (row_loss, col_loss)

    return jax.shard_map(
        on_device,
        mesh=mesh,
        in_specs=(P("dp", "mp", None), P("dp", None), P()),
        out_specs=(P("dp", "mp"), P("dp", "mp")),
        check_vma=False,
    )
```

```python
import functools

import jax
import jax.numpy as jnp
from jax import lax
from jax.experimental import pallas as pl
from jax.experimental.pallas import tpu as pltpu
from jax.sharding import PartitionSpec as P

MESH = pl.DeviceIdType.MESH
F32 = jnp.float32
IMG_PARTS = 4
TXT_PARTS = 2


def normalize(raw):
    wide = raw.astype(F32)
    total = jnp.sum(wide * wide, axis=1, keepdims=True)
    return (wide * lax.rsqrt(total + 1e-06)).astype(jnp.bfloat16)


def lane_sums(values):
    folded = values[:, :128]
    for start in range(128, values.shape[1], 128):
        folded = folded + values[:, start : start + 128]
    return jnp.sum(folded.T, axis=0, keepdims=True)


def flipped(index, mask):
    bit = 1
    while bit <= mask:
        if mask & bit:
            index = index + bit * (1 - 2 * (index // bit % 2))
        bit *= 2
    return index


def kernel(
    groups, run, ring,
    scale_ref, image_ref, text_ref, out_ref,
    image_own, img_raw, txt_raw, img_n, txt_n, weights_col, row_out, row_in, col_out, col_in,
    local_sem, img_send, img_recv, txt_send, txt_recv, row_send, row_recv, col_send, col_recv,
):
    group = lax.axis_index("mp")
    me = lax.axis_index("dp")
    rows = image_ref.shape[0]
    cols = text_ref.shape[0]
    lane = me % run
    spot = me // run

    def along(step):
        return ((spot + step + ring) % ring) * run + lane

    def remote(src, dst, send, recv, dp, mp=None):
        where = {"dp": dp} if mp is None else {"dp": dp, "mp": mp}
        return pltpu.make_async_remote_copy(
            src_ref=src, dst_ref=dst, send_sem=send, recv_sem=recv,
            device_id=where, device_id_type=MESH,
        )

    load_img = pltpu.make_async_copy(image_ref, image_own, local_sem.at[0])
    load_txt = pltpu.make_async_copy(text_ref, txt_raw.at[0], local_sem.at[1])
    load_img.start()
    load_txt.start()

    barrier = pltpu.get_barrier_semaphore()
    greeted = 0
    for step in range(1, ring):
        pl.semaphore_signal(barrier, inc=1, device_id={"dp": along(step)}, device_id_type=MESH)
        greeted += 1
    for k in range(run):
        for m in range(groups):
            if k or m:
                pl.semaphore_signal(
                    barrier, inc=1, device_id_type=MESH,
                    device_id={"dp": flipped(me, k), "mp": (group + m) % groups},
                )
                greeted += 1
    pl.semaphore_wait(barrier, greeted)

    part_rows = rows // IMG_PARTS

    def img_copy(way, source, part, own=False):
        span = pl.ds(part * part_rows, part_rows)
        return remote(
            image_ref.at[span] if own else img_raw.at[source, span],
            img_raw.at[source, span],
            img_send.at[way, source, part], img_recv.at[source, part],
            along(1 - 2 * way),
        )

    def pass_on(source, part, own=False, ended=False):
        for way in range(2):
            if own:
                goes = spot < ring - 1 if way == 0 else spot > 0
            elif way == 0:
                goes = jnp.logical_and(source < spot, spot < ring - 1)
            else:
                goes = jnp.logical_and(source > spot, spot > 0)
            copy = img_copy(way, source, part, own)

            @pl.when(goes)
            def _():
                copy.wait_send() if ended else copy.start()

    short = jnp.minimum(spot, ring - 1 - spot)
    ahead = jnp.where(spot < ring - 1 - spot, 1, -1)

    def nearest(turn):
        both = (turn + 1) // 2 * (1 - 2 * (turn % 2))
        return spot + jnp.where(turn <= 2 * short, both, ahead * (turn - short))

    txt_rows = cols // TXT_PARTS

    def txt_copy(slot, part):
        bit = slot & -slot
        held = slot - bit
        span = pl.ds(part * txt_rows, txt_rows)
        return remote(
            txt_raw.at[held, span] if held else text_ref.at[span],
            txt_raw.at[slot, span],
            txt_send.at[slot - 1, part], txt_recv.at[slot - 1, part], flipped(me, bit),
        )

    txt_sent = []

    def txt_start(slot, part):
        copy = txt_copy(slot, part)
        copy.start()
        txt_sent.append(copy)

    def txt_arrive(slot, part):
        txt_copy(slot, part).wait_recv()
        bit = 1
        while bit < slot & -slot:
            txt_start(slot + bit, part)
            bit *= 2

    def txt_block(slot):
        txt_n[pl.ds(slot * cols, cols)] = normalize(txt_raw[slot])

    for part in range(IMG_PARTS):
        pass_on(spot, part, True)
    for slot in reversed(range(1, run)):
        if slot & (slot - 1) == 0:
            for part in range(TXT_PARTS):
                txt_start(slot, part)

    scale = scale_ref[0]
    load_img.wait()
    load_txt.wait()
    img_n[0] = normalize(image_own[...])
    txt_n[pl.ds(0, cols)] = normalize(txt_raw[0])
    own = txt_n[pl.ds(pl.multiple_of(group * rows, rows), rows)]
    diag = scale * lane_sums(img_n[0].astype(F32) * own.astype(F32))

    def img_arrive(turn, part):
        source = nearest(turn)
        img_copy(0, source, part).wait_recv()
        pass_on(source, part)

    def img_block(turn):
        img_n[turn] = normalize(img_raw[nearest(turn)])

    txt_order = sorted(range(1, run), key=lambda k: -(k & -k))
    txt_waits = [(slot, part) for slot in txt_order if slot % 2 == 0 for part in range(TXT_PARTS)]
    img_waits = [
        (turn, part)
        for pair in range(1, ring, 2)
        for part in range(IMG_PARTS)
        for turn in range(pair, min(pair + 2, ring))
    ]
    at_end = jnp.logical_or(spot == 0, spot == ring - 1)

    def img_early(turn, part):
        if turn < ring - 1:
            img_arrive(turn, part)
        else:

            @pl.when(jnp.logical_not(at_end))
            def _():
                img_arrive(turn, part)

    lead = min(2 * IMG_PARTS, len(img_waits))
    for turn, part in img_waits[:lead]:
        img_early(turn, part)
    rest = img_waits[lead:]
    share = -(-len(rest) // max(len(txt_waits) - 1, 1))
    for i in range(max(len(txt_waits), 1)):
        for slot, part in txt_waits[i : i + 1]:
            txt_arrive(slot, part)
        for turn, part in rest[i * share : (i + 1) * share]:
            img_early(turn, part)
    for slot in txt_order:
        if slot % 2 == 0:
            txt_block(slot)
    for turn in range(1, ring - 1):
        img_block(turn)
    for slot in txt_order:
        if slot % 2:
            for part in range(TXT_PARTS):
                txt_arrive(slot, part)
            txt_block(slot)

    row_copies = []

    def image_rows(turn):
        scores = scale * lax.dot_general(
            img_n[turn], txt_n[...], (((1,), (1,)), ((), ())), preferred_element_type=F32
        )
        weights = jnp.exp(scores)
        sums = jnp.broadcast_to(lane_sums(weights), (8, rows))
        if turn == 0:
            row_in[spot, :, :rows] = sums
        else:
            row_out[turn, :, :rows] = sums
            copy = remote(
                row_out.at[turn], row_in.at[spot],
                row_send.at[turn - 1], row_recv.at[spot],
                nearest(turn) * run + lane,
            )
            copy.start()
            row_copies.append(copy)
        part = jnp.sum(weights, axis=0, keepdims=True)
        weights_col[...] = part if turn == 0 else weights_col[...] + part

    for turn in range(ring - 1):
        image_rows(turn)
    for part in range(IMG_PARTS):

        @pl.when(at_end)
        def _():
            img_copy(0, nearest(ring - 1), part).wait_recv()

    img_block(ring - 1)
    image_rows(ring - 1)

    col_copies = []
    for k in range(run):
        col_out[k] = jnp.broadcast_to(weights_col[:, k * cols : (k + 1) * cols], (8, cols))
        for m in range(groups):
            if k or m:
                to = k * groups + (groups - m) % groups
                copy = remote(
                    col_out.at[k], col_in.at[to],
                    col_send.at[k * groups + m], col_recv.at[to],
                    flipped(me, k), (group + m) % groups,
                )
                copy.start()
                col_copies.append(copy)
    for turn in range(1, ring):
        source = nearest(turn)
        remote(
            row_out.at[turn], row_in.at[source], row_send.at[turn - 1], row_recv.at[source],
            source * run + lane,
        ).wait_recv()
    row_total = row_in[0, :1, :rows]
    for slot in range(1, ring):
        row_total = row_total + row_in[slot, :1, :rows]
    for copy in col_copies:
        copy.wait_recv()
    col_total = col_out[0, :1]
    for slot in range(1, run * groups):
        col_total = col_total + col_in[slot, :1]
    col_own = col_total[:, :rows]
    for g in range(1, groups):
        col_own = jnp.where(group == g, col_total[:, g * rows : (g + 1) * rows], col_own)
    out_ref[0:1] = row_total
    out_ref[1:2] = col_own
    out_ref[2:3] = diag
    for part in range(IMG_PARTS):
        pass_on(spot, part, True, True)
        for turn in range(1, ring):
            pass_on(nearest(turn), part, False, True)
    for copy in [*txt_sent, *row_copies, *col_copies]:
        copy.wait_send()


def solution(mesh):
    groups, n = mesh.shape["mp"], mesh.shape["dp"]
    run = 1 << ((n.bit_length() - 1) // 2)
    ring = n // run

    def on_device(image, text, logit_scale):
        _, rows, depth = image.shape
        cols = text.shape[0]
        hbm = pl.BlockSpec(memory_space=pl.ANY)
        dma = pltpu.SemaphoreType.DMA
        totals = pl.pallas_call(
            functools.partial(kernel, groups, run, ring),
            out_shape=jax.ShapeDtypeStruct((3, rows), F32),
            in_specs=[pl.BlockSpec(memory_space=pltpu.SMEM), hbm, hbm],
            out_specs=pl.BlockSpec(memory_space=pltpu.VMEM),
            scratch_shapes=[
                pltpu.VMEM((rows, depth), jnp.bfloat16),
                pltpu.VMEM((ring, rows, depth), jnp.bfloat16),
                pltpu.VMEM((run, cols, depth), jnp.bfloat16),
                pltpu.VMEM((ring, rows, depth), jnp.bfloat16),
                pltpu.VMEM((run * cols, depth), jnp.bfloat16),
                pltpu.VMEM((1, run * cols), F32),
                pltpu.VMEM((ring, 8, 128), F32),
                pltpu.VMEM((ring, 8, 128), F32),
                pltpu.VMEM((run, 8, cols), F32),
                pltpu.VMEM((run * groups, 8, cols), F32),
                dma((2,)),
                dma((2, ring, IMG_PARTS)),
                dma((ring, IMG_PARTS)),
                dma((run - 1, TXT_PARTS)),
                dma((run - 1, TXT_PARTS)),
                dma((ring - 1,)),
                dma((ring,)),
                dma((run * groups,)),
                dma((run * groups,)),
            ],
            compiler_params=pltpu.CompilerParams(collective_id=0, has_side_effects=True),
        )(logit_scale, image.reshape(rows, depth), text)
        row_loss = jnp.log(totals[0:1]) - totals[2:3]
        col_loss = jnp.log(totals[1:2]) - totals[2:3]
        return (row_loss, col_loss)

    return jax.shard_map(
        on_device,
        mesh=mesh,
        in_specs=(P("dp", "mp", None), P("dp", None), P()),
        out_specs=(P("dp", "mp"), P("dp", "mp")),
        check_vma=False,
    )
```

```python
import functools

import jax
import jax.numpy as jnp
from jax import lax
from jax.experimental import pallas as pl
from jax.experimental.pallas import tpu as pltpu
from jax.sharding import PartitionSpec as P

MESH = pl.DeviceIdType.MESH
F32 = jnp.float32


def normalize(raw):
    wide = raw.astype(F32)
    total = jnp.sum(wide * wide, axis=1, keepdims=True)
    return (wide * lax.rsqrt(total + 1e-06)).astype(jnp.bfloat16)


def lane_sums(values):
    folded = values[:, :128]
    for start in range(128, values.shape[1], 128):
        folded = folded + values[:, start : start + 128]
    return jnp.sum(folded.T, axis=0, keepdims=True)


def flipped(index, mask):
    bit = 1
    while bit <= mask:
        if mask & bit:
            index = index + bit * (1 - 2 * (index // bit % 2))
        bit *= 2
    return index


def kernel(
    groups, run, ring,
    scale_ref, image_ref, text_ref, out_ref,
    img_raw, txt_raw, img_n, txt_n, weights_col, row_out, row_in, col_out, col_in,
    local_sem, img_send, img_recv, txt_send, txt_recv, row_send, row_recv, col_send, col_recv,
):
    group = lax.axis_index("mp")
    me = lax.axis_index("dp")
    rows = image_ref.shape[0]
    cols = text_ref.shape[0]
    half = rows // 2
    lane = me % run
    spot = me // run

    def along(step):
        return ((spot + step + ring) % ring) * run + lane

    def remote(src, dst, send, recv, dp, mp=None):
        where = {"dp": dp} if mp is None else {"dp": dp, "mp": mp}
        return pltpu.make_async_remote_copy(
            src_ref=src, dst_ref=dst, send_sem=send, recv_sem=recv,
            device_id=where, device_id_type=MESH,
        )

    load_img = pltpu.make_async_copy(image_ref, img_raw.at[0], local_sem.at[0])
    load_txt = pltpu.make_async_copy(text_ref, txt_raw.at[0], local_sem.at[1])
    load_img.start()
    load_txt.start()

    barrier = pltpu.get_barrier_semaphore()
    greeted = 0
    for step in range(1, ring):
        pl.semaphore_signal(barrier, inc=1, device_id={"dp": along(step)}, device_id_type=MESH)
        greeted += 1
    for k in range(run):
        for m in range(groups):
            if k or m:
                pl.semaphore_signal(
                    barrier, inc=1, device_id_type=MESH,
                    device_id={"dp": flipped(me, k), "mp": (group + m) % groups},
                )
                greeted += 1
    pl.semaphore_wait(barrier, greeted)

    def img_copy(way, step, part):
        held = (ring - (step - 1)) % ring if way == 0 else step - 1
        lands = ring - step if way == 0 else step
        span = pl.ds(part * half, half)
        src = image_ref.at[span] if step == 1 else img_raw.at[held, span]
        return remote(
            src, img_raw.at[lands, span],
            img_send.at[way, step - 1, part], img_recv.at[way, step - 1, part],
            along(1 if way == 0 else -1),
        )

    last = ring // 2
    img_copies = {}
    for step in range(1, last + 1):
        for way in range(2):
            for part in ((0, 1) if way == 0 else (1, 0)):
                if step < last or part == way:
                    img_copies[way, step, part] = img_copy(way, step, part)

    def txt_copy(slot):
        bit = slot & -slot
        held = slot - bit
        src = text_ref if held == 0 else txt_raw.at[held]
        return remote(
            src, txt_raw.at[slot], txt_send.at[slot - 1], txt_recv.at[slot - 1],
            flipped(me, bit),
        )

    txt_copies = {slot: txt_copy(slot) for slot in range(1, run)}

    for key in img_copies:
        if key[1] == 1:
            img_copies[key].start()
    for slot in reversed(range(1, run)):
        if slot & (slot - 1) == 0:
            txt_copies[slot].start()

    scale = scale_ref[0]
    load_img.wait()
    load_txt.wait()
    img_n[0] = normalize(img_raw[0])
    txt_n[pl.ds(0, cols)] = normalize(txt_raw[0])
    own = txt_n[pl.ds(pl.multiple_of(group * rows, rows), rows)]
    diag = scale * lane_sums(img_n[0].astype(F32) * own.astype(F32))

    def img_arrive(way, step, part):
        img_copies[way, step, part].wait_recv()
        if (way, step + 1, part) in img_copies:
            img_copies[way, step + 1, part].start()

    for step in range(1, last):
        for order in range(2):
            for way in range(2):
                img_arrive(way, step, way if order == 0 else 1 - way)
        for slot in (step, ring - step):
            img_n[slot] = normalize(img_raw[slot])

    for bit in reversed(range(run.bit_length() - 1)):
        for slot in range(1, run):
            if slot & -slot == 1 << bit:
                txt_copies[slot].wait_recv()
                for low in range(bit):
                    txt_copies[slot + (1 << low)].start()
                txt_n[pl.ds(slot * cols, cols)] = normalize(txt_raw[slot])

    order = [0]
    for step in range(1, last):
        order += [step, ring - step]
    order.append(last)
    row_copies = []
    for turn, slot in enumerate(order):
        if slot == last:
            for way in range(2):
                img_arrive(way, last, way)
            img_n[last] = normalize(img_raw[last])
        scores = scale * lax.dot_general(
            img_n[slot], txt_n[...], (((1,), (1,)), ((), ())), preferred_element_type=F32
        )
        weights = jnp.exp(scores)
        sums = lane_sums(weights)
        if slot == 0:
            row_in[0, :, :rows] = jnp.broadcast_to(sums, (8, rows))
        else:
            row_out[slot, :, :rows] = jnp.broadcast_to(sums, (8, rows))
            copy = remote(
                row_out.at[slot], row_in.at[ring - slot],
                row_send.at[slot - 1], row_recv.at[ring - slot - 1], along(slot),
            )
            copy.start()
            row_copies.append(copy)
        part = jnp.sum(weights, axis=0, keepdims=True)
        weights_col[...] = part if turn == 0 else weights_col[...] + part

    col_copies = []
    for k in range(run):
        col_out[k] = jnp.broadcast_to(weights_col[:, k * cols : (k + 1) * cols], (8, cols))
        for m in range(groups):
            if k or m:
                copy = remote(
                    col_out.at[k], col_in.at[k * groups + (groups - m) % groups],
                    col_send.at[k * groups + m], col_recv.at[k * groups + (groups - m) % groups],
                    flipped(me, k), (group + m) % groups,
                )
                copy.start()
                col_copies.append(copy)
    row_total = row_in[0, :1, :rows]
    for copy in row_copies:
        copy.wait_recv()
    for slot in range(1, ring):
        row_total = row_total + row_in[slot, :1, :rows]
    out_ref[0:1] = row_total
    out_ref[2:3] = diag
    for copy in col_copies:
        copy.wait_recv()
    col_total = col_out[0, :1]
    for slot in range(1, run * groups):
        col_total = col_total + col_in[slot, :1]
    col_own = col_total[:, :rows]
    for g in range(1, groups):
        col_own = jnp.where(group == g, col_total[:, g * rows : (g + 1) * rows], col_own)
    out_ref[1:2] = col_own
    for copy in [*img_copies.values(), *txt_copies.values(), *row_copies, *col_copies]:
        copy.wait_send()


def solution(mesh):
    groups, n = mesh.shape["mp"], mesh.shape["dp"]
    run = 1 << ((n.bit_length() - 1) // 2)
    ring = n // run

    def on_device(image, text, logit_scale):
        _, rows, depth = image.shape
        cols = text.shape[0]
        vmem = pl.BlockSpec(memory_space=pltpu.VMEM)
        hbm = pl.BlockSpec(memory_space=pl.ANY)
        dma = pltpu.SemaphoreType.DMA
        totals = pl.pallas_call(
            functools.partial(kernel, groups, run, ring),
            out_shape=jax.ShapeDtypeStruct((3, rows), F32),
            in_specs=[pl.BlockSpec(memory_space=pltpu.SMEM), hbm, hbm],
            out_specs=vmem,
            scratch_shapes=[
                pltpu.VMEM((ring, rows, depth), jnp.bfloat16),
                pltpu.VMEM((run, cols, depth), jnp.bfloat16),
                pltpu.VMEM((ring, rows, depth), jnp.bfloat16),
                pltpu.VMEM((run * cols, depth), jnp.bfloat16),
                pltpu.VMEM((1, run * cols), F32),
                pltpu.VMEM((ring, 8, 128), F32),
                pltpu.VMEM((ring, 8, 128), F32),
                pltpu.VMEM((run, 8, cols), F32),
                pltpu.VMEM((run * groups, 8, cols), F32),
                dma((2,)),
                dma((2, ring // 2, 2)),
                dma((2, ring // 2, 2)),
                dma((run - 1,)),
                dma((run - 1,)),
                dma((ring - 1,)),
                dma((ring - 1,)),
                dma((run * groups,)),
                dma((run * groups,)),
            ],
            compiler_params=pltpu.CompilerParams(collective_id=0, has_side_effects=True),
        )(logit_scale, image.reshape(rows, depth), text)
        row_loss = jnp.log(totals[0:1]) - totals[2:3]
        col_loss = jnp.log(totals[1:2]) - totals[2:3]
        return (row_loss, col_loss)

    return jax.shard_map(
        on_device,
        mesh=mesh,
        in_specs=(P("dp", "mp", None), P("dp", None), P()),
        out_specs=(P("dp", "mp"), P("dp", "mp")),
        check_vma=False,
    )
```

```python
import functools

import jax
import jax.numpy as jnp
from jax import lax
from jax.experimental import pallas as pl
from jax.experimental.pallas import tpu as pltpu
from jax.sharding import PartitionSpec as P

MESH = pl.DeviceIdType.MESH
F32 = jnp.float32
IMG_PARTS = 2
TXT_PARTS = 1


def normalize(raw):
    wide = raw.astype(F32)
    total = jnp.sum(wide * wide, axis=1, keepdims=True)
    return (wide * lax.rsqrt(total + 1e-06)).astype(jnp.bfloat16)


def lane_sums(values):
    folded = values[:, :128]
    for start in range(128, values.shape[1], 128):
        folded = folded + values[:, start : start + 128]
    return jnp.sum(folded.T, axis=0, keepdims=True)


def flipped(index, mask):
    bit = 1
    while bit <= mask:
        if mask & bit:
            index = index + bit * (1 - 2 * (index // bit % 2))
        bit *= 2
    return index


def kernel(
    groups, run, ring,
    scale_ref, image_ref, text_ref, out_ref,
    image_own, img_raw, txt_raw, img_n, txt_n, weights_col, row_out, row_in, col_out, col_in,
    local_sem, img_send, img_recv, txt_send, txt_recv, row_send, row_recv, col_send, col_recv,
):
    group = lax.axis_index("mp")
    me = lax.axis_index("dp")
    rows = image_ref.shape[0]
    cols = text_ref.shape[0]
    lane = me % run
    spot = me // run

    def along(step):
        return ((spot + step + ring) % ring) * run + lane

    def remote(src, dst, send, recv, dp, mp=None):
        where = {"dp": dp} if mp is None else {"dp": dp, "mp": mp}
        return pltpu.make_async_remote_copy(
            src_ref=src, dst_ref=dst, send_sem=send, recv_sem=recv,
            device_id=where, device_id_type=MESH,
        )

    load_img = pltpu.make_async_copy(image_ref, image_own, local_sem.at[0])
    load_txt = pltpu.make_async_copy(text_ref, txt_raw.at[0], local_sem.at[1])
    load_img.start()
    load_txt.start()

    barrier = pltpu.get_barrier_semaphore()
    greeted = 0
    for step in range(1, ring):
        pl.semaphore_signal(barrier, inc=1, device_id={"dp": along(step)}, device_id_type=MESH)
        greeted += 1
    for k in range(run):
        for m in range(groups):
            if k or m:
                pl.semaphore_signal(
                    barrier, inc=1, device_id_type=MESH,
                    device_id={"dp": flipped(me, k), "mp": (group + m) % groups},
                )
                greeted += 1
    pl.semaphore_wait(barrier, greeted)

    part_rows = rows // IMG_PARTS

    def img_copy(way, source, part, own=False):
        span = pl.ds(part * part_rows, part_rows)
        return remote(
            image_ref.at[span] if own else img_raw.at[source, span],
            img_raw.at[source, span],
            img_send.at[way, source, part], img_recv.at[source, part],
            along(1 - 2 * way),
        )

    def pass_on(source, part, own=False, ended=False):
        for way in range(2):
            if own:
                goes = spot < ring - 1 if way == 0 else spot > 0
            elif way == 0:
                goes = jnp.logical_and(source < spot, spot < ring - 1)
            else:
                goes = jnp.logical_and(source > spot, spot > 0)
            copy = img_copy(way, source, part, own)

            @pl.when(goes)
            def _():
                copy.wait_send() if ended else copy.start()

    short = jnp.minimum(spot, ring - 1 - spot)
    ahead = jnp.where(spot < ring - 1 - spot, 1, -1)

    def nearest(turn):
        both = (turn + 1) // 2 * (1 - 2 * (turn % 2))
        return spot + jnp.where(turn <= 2 * short, both, ahead * (turn - short))

    txt_rows = cols // TXT_PARTS

    def txt_copy(slot, part):
        bit = slot & -slot
        held = slot - bit
        span = pl.ds(part * txt_rows, txt_rows)
        return remote(
            txt_raw.at[held, span] if held else text_ref.at[span],
            txt_raw.at[slot, span],
            txt_send.at[slot - 1, part], txt_recv.at[slot - 1, part], flipped(me, bit),
        )

    txt_sent = []

    def txt_start(slot, part):
        copy = txt_copy(slot, part)
        copy.start()
        txt_sent.append(copy)

    def txt_arrive(slot, part):
        txt_copy(slot, part).wait_recv()
        bit = 1
        while bit < slot & -slot:
            txt_start(slot + bit, part)
            bit *= 2

    def txt_block(slot):
        txt_n[pl.ds(slot * cols, cols)] = normalize(txt_raw[slot])

    for part in range(IMG_PARTS):
        pass_on(spot, part, True)
    for slot in reversed(range(1, run)):
        if slot & (slot - 1) == 0:
            for part in range(TXT_PARTS):
                txt_start(slot, part)

    scale = scale_ref[0]
    load_img.wait()
    load_txt.wait()
    img_n[0] = normalize(image_own[...])
    txt_n[pl.ds(0, cols)] = normalize(txt_raw[0])
    own = txt_n[pl.ds(pl.multiple_of(group * rows, rows), rows)]
    diag = scale * lane_sums(img_n[0].astype(F32) * own.astype(F32))

    def img_arrive(turn, part):
        source = nearest(turn)
        img_copy(0, source, part).wait_recv()
        pass_on(source, part)

    def img_block(turn):
        img_n[turn] = normalize(img_raw[nearest(turn)])

    txt_order = sorted(range(1, run), key=lambda k: -(k & -k))
    txt_waits = [(slot, part) for slot in txt_order if slot % 2 == 0 for part in range(TXT_PARTS)]
    img_waits = [
        (turn, part)
        for pair in range(1, ring, 2)
        for part in range(IMG_PARTS)
        for turn in range(pair, min(pair + 2, ring))
    ]
    at_end = jnp.logical_or(spot == 0, spot == ring - 1)

    def img_early(turn, part):
        if turn < ring - 1:
            img_arrive(turn, part)
        else:

            @pl.when(jnp.logical_not(at_end))
            def _():
                img_arrive(turn, part)

    for turn, part in img_waits[: 2 * IMG_PARTS]:
        if turn == 1:
            img_arrive(turn, part)
        else:

            @pl.when(jnp.logical_not(at_end))
            def _():
                img_arrive(turn, part)

    for turn, part in img_waits[2 * IMG_PARTS :]:

        @pl.when(jnp.logical_not(at_end))
        def _():
            img_arrive(turn, part)

    for slot, part in txt_waits:
        txt_arrive(slot, part)
    for turn, part in img_waits:
        if 1 < turn < ring - 1:

            @pl.when(at_end)
            def _():
                img_arrive(turn, part)

    for slot in txt_order:
        if slot % 2 == 0:
            txt_block(slot)
    for turn in range(1, ring - 1):
        img_block(turn)
    for slot in txt_order:
        if slot % 2:
            for part in range(TXT_PARTS):
                txt_arrive(slot, part)
            txt_block(slot)

    row_copies = []

    def image_weights(first, count):
        block = img_n[pl.ds(first, count)].reshape(count * rows, -1)
        scores = scale * lax.dot_general(
            block, txt_n[...], (((1,), (1,)), ((), ())), preferred_element_type=F32
        )
        return jnp.exp(scores)

    def image_rows(turn, weights):
        sums = jnp.broadcast_to(lane_sums(weights), (8, rows))
        if turn == 0:
            row_in[spot, :, :rows] = sums
        else:
            row_out[turn, :, :rows] = sums
            copy = remote(
                row_out.at[turn], row_in.at[spot],
                row_send.at[turn - 1], row_recv.at[spot],
                nearest(turn) * run + lane,
            )
            copy.start()
            row_copies.append(copy)
        part = jnp.sum(weights, axis=0, keepdims=True)
        weights_col[...] = part if turn == 0 else weights_col[...] + part

    early = image_weights(0, ring - 1)
    for turn in range(ring - 1):
        image_rows(turn, early[turn * rows : (turn + 1) * rows])
    for part in range(IMG_PARTS):

        @pl.when(at_end)
        def _():
            img_copy(0, nearest(ring - 1), part).wait_recv()

    img_block(ring - 1)
    image_rows(ring - 1, image_weights(ring - 1, 1))

    col_copies = []
    for k in range(run):
        col_out[k] = jnp.broadcast_to(weights_col[:, k * cols : (k + 1) * cols], (8, cols))
        for m in range(groups):
            if k or m:
                to = k * groups + (groups - m) % groups
                copy = remote(
                    col_out.at[k], col_in.at[to],
                    col_send.at[k * groups + m], col_recv.at[to],
                    flipped(me, k), (group + m) % groups,
                )
                copy.start()
                col_copies.append(copy)
    for turn in range(1, ring):
        source = nearest(turn)
        remote(
            row_out.at[turn], row_in.at[source], row_send.at[turn - 1], row_recv.at[source],
            source * run + lane,
        ).wait_recv()
    row_total = row_in[0, :1, :rows]
    for slot in range(1, ring):
        row_total = row_total + row_in[slot, :1, :rows]
    for copy in col_copies:
        copy.wait_recv()
    col_total = col_out[0, :1]
    for slot in range(1, run * groups):
        col_total = col_total + col_in[slot, :1]
    col_own = col_total[:, :rows]
    for g in range(1, groups):
        col_own = jnp.where(group == g, col_total[:, g * rows : (g + 1) * rows], col_own)
    out_ref[0:1] = row_total
    out_ref[1:2] = col_own
    out_ref[2:3] = diag
    for part in range(IMG_PARTS):
        pass_on(spot, part, True, True)
        for turn in range(1, ring):
            pass_on(nearest(turn), part, False, True)
    for copy in [*txt_sent, *row_copies, *col_copies]:
        copy.wait_send()


def solution(mesh):
    groups, n = mesh.shape["mp"], mesh.shape["dp"]
    run = 1 << ((n.bit_length() - 1) // 2)
    ring = n // run

    def on_device(image, text, logit_scale):
        _, rows, depth = image.shape
        cols = text.shape[0]
        hbm = pl.BlockSpec(memory_space=pl.ANY)
        dma = pltpu.SemaphoreType.DMA
        totals = pl.pallas_call(
            functools.partial(kernel, groups, run, ring),
            out_shape=jax.ShapeDtypeStruct((3, rows), F32),
            in_specs=[pl.BlockSpec(memory_space=pltpu.SMEM), hbm, hbm],
            out_specs=pl.BlockSpec(memory_space=pltpu.VMEM),
            scratch_shapes=[
                pltpu.VMEM((rows, depth), jnp.bfloat16),
                pltpu.VMEM((ring, rows, depth), jnp.bfloat16),
                pltpu.VMEM((run, cols, depth), jnp.bfloat16),
                pltpu.VMEM((ring, rows, depth), jnp.bfloat16),
                pltpu.VMEM((run * cols, depth), jnp.bfloat16),
                pltpu.VMEM((1, run * cols), F32),
                pltpu.VMEM((ring, 8, 128), F32),
                pltpu.VMEM((ring, 8, 128), F32),
                pltpu.VMEM((run, 8, cols), F32),
                pltpu.VMEM((run * groups, 8, cols), F32),
                dma((2,)),
                dma((2, ring, IMG_PARTS)),
                dma((ring, IMG_PARTS)),
                dma((run - 1, TXT_PARTS)),
                dma((run - 1, TXT_PARTS)),
                dma((ring - 1,)),
                dma((ring,)),
                dma((run * groups,)),
                dma((run * groups,)),
            ],
            compiler_params=pltpu.CompilerParams(collective_id=0, has_side_effects=True),
        )(logit_scale, image.reshape(rows, depth), text)
        row_loss = jnp.log(totals[0:1]) - totals[2:3]
        col_loss = jnp.log(totals[1:2]) - totals[2:3]
        return (row_loss, col_loss)

    return jax.shard_map(
        on_device,
        mesh=mesh,
        in_specs=(P("dp", "mp", None), P("dp", None), P()),
        out_specs=(P("dp", "mp"), P("dp", "mp")),
        check_vma=False,
    )
```
